32 devices in a mesh: groups: 2 (over y), seq: 4 (over z), cell: 4 (over x, core).
Axes of the slice: x: 2, y: 2, z: 4, core: 2. Of those that a mesh axis runs over, the one named last changes fastest.
Arguments:
- dna_bases: int32 [65536], P(('groups', 'seq')), parts along dimension 0, may hold values from 0 to 3
- stem_weight: bfloat16 [512, 768], replicated, may hold values from -0.5 to 0.5
- conv_weight: bfloat16 [2, 384, 3, 768], P(None, 'cell'), may hold values from -0.125 to 0.125
- proj_weight: bfloat16 [2, 384, 768], P(None, 'cell'), may hold values from -0.3125 to 0.3125
- emission_head_weight: bfloat16 [32, 768, 128], P('cell'), may hold values from -0.046875 to 0.046875
- transitions: float32 [32, 128, 128], P('cell'), may hold values from -1 to 109
Outputs:
- log_marginals: float32 [32, 512, 128], P('cell', ('groups', 'seq')), parts along dimension 1
The draws below stay inside these ranges and needn't reach their ends.
There are 2 independent parts, one for each index of `groups`. The reference program is written for one: setup_inputs(seed, part) draws one part's arguments, and reference() takes and returns one part's arrays. A program takes and returns all parts, laid end to end along the dimension named above; an argument that names none is the same for every part. Nothing has to cross between parts.
All inputs are finite; a program needn't handle non-finite values.
Results may differ from the reference program's by a relative error of at most 0.0007.
Values may be sent and summed in bfloat16 or wider, within the bound.
A program may use at most 128 MiB of HBM per device.

```python
import jax
import jax.numpy as jnp
from jax import lax

D = 768
INNER = 384
LABEL_COUNT = 128
TISSUE_TYPES = 32
BIN_BP = 128
LAYERS = 2
BASE_DILATION = 4
BINS = 256


def draw_transitions(key, part):
    noise_key = jax.random.fold_in(key, 7)
    persistence_random_seed = jax.random.fold_in(key, 13)
    cross_label_mask = jax.random.uniform(noise_key, (TISSUE_TYPES, LABEL_COUNT, LABEL_COUNT), jnp.float32, -1.0, 1.0)
    persistence_reward = jax.random.uniform(persistence_random_seed, (TISSUE_TYPES, 1, 1), jnp.float32, 8.0, 14.0)
    return cross_label_mask + persistence_reward * jnp.eye(LABEL_COUNT, dtype=jnp.float32)


def place_ends(values, stream_key, low, top_value):
    extent = values.shape
    place = [jax.random.randint(jax.random.fold_in(stream_key, axis), (), 0, extent[axis]) for axis in range(len(extent))]
    values = values.at[tuple(place)].set(low)
    longest = extent.index(max(extent))
    place[longest] = (place[longest] + 1) % extent[longest]
    return values.at[tuple(place)].set(top_value)


def shard_levels(key, extent, shards, smallest, top_value):
    def one(dim, shards_of):
        draws = jax.random.uniform(jax.random.fold_in(jax.random.fold_in(key, 6), dim), (shards_of,), jnp.float32, smallest / len(shards), top_value / len(shards))
        return jnp.repeat(jnp.exp(draws), extent[dim] // shards_of).reshape((-1,) + (1,) * (len(extent) - dim - 1))

    level = one(*shards[0])
    for cut in shards[1:]:
        level = level * one(*cut)
    return level


def noise(stream_key, extent, scale, limit, split=(), held_as=jnp.bfloat16):
    array = jax.random.normal(stream_key, extent, jnp.float32) * scale
    if len(split) > 0:
        array = shard_levels(stream_key, extent, split, -0.22, 0.18) * array
    return jnp.clip(array, min=-limit, max=limit).astype(held_as)


def setup_inputs(seed: int = 0, part: int = 0) -> dict:
    arg_keys = jax.random.split(jax.random.key(seed), 7)
    own_keys = jax.random.split(jax.random.fold_in(arg_keys[6], part), 7)
    return {
        "dna_bases": place_ends(jax.random.randint(own_keys[0], (BINS * BIN_BP,), 0, 4), jax.random.fold_in(own_keys[0], 1), 0, 3).astype(jnp.int32),
        "stem_weight": noise(arg_keys[1], (BIN_BP * 4, D), BIN_BP ** -0.5, 0.5),
        "conv_weight": noise(arg_keys[2], (LAYERS, INNER, 3, D), (3 * D) ** -0.5, 0.125, ((1, 4),)),
        "proj_weight": noise(arg_keys[3], (LAYERS, INNER, D), INNER ** -0.5, 0.3125, ((1, 4),)),
        "emission_head_weight": noise(arg_keys[4], (TISSUE_TYPES, D, LABEL_COUNT), (25 * D) ** -0.5, 0.046875, ((0, 4),)),
        "transitions": draw_transitions(jax.random.fold_in(arg_keys[6], 71), part),
    }


def scaled(values):
    return values * lax.rsqrt(lax.optimization_barrier(jnp.mean(values * values, axis=-1, keepdims=True)) + 1e-06)

def reference(dna_bases, stem_weight, conv_weight, proj_weight, emission_head_weight, transitions):
    base_hits = dna_bases.reshape(BINS, BIN_BP, 1) == jnp.arange(4, dtype=jnp.int32)
    one_hot = base_hits.astype(jnp.bfloat16).reshape(BINS, BIN_BP * 4)
    stem_out = jnp.dot(one_hot, stem_weight, preferred_element_type=jnp.float32).astype(jnp.bfloat16)
    residual = stem_out.astype(jnp.float32)
    for layer_position in range(LAYERS):
        spacing_multiplier = BASE_DILATION * 2 ** layer_position
        conv_input = jax.nn.gelu(scaled(residual)).astype(jnp.bfloat16)
        padded = jnp.pad(conv_input, ((spacing_multiplier, spacing_multiplier), (0, 0)))
        stacked = jnp.concatenate([padded[0:BINS], padded[spacing_multiplier:spacing_multiplier + BINS], padded[2 * spacing_multiplier:2 * spacing_multiplier + BINS]], axis=1)
        flat_weight = conv_weight[layer_position].reshape(INNER, 3 * D)
        conv_out = jnp.dot(stacked, flat_weight.T, preferred_element_type=jnp.float32)
        hidden = jax.nn.gelu(conv_out).astype(jnp.bfloat16)
        residual = residual + jnp.dot(hidden, proj_weight[layer_position], preferred_element_type=jnp.float32)
    trunk_features = scaled(residual).astype(jnp.bfloat16)
    emission_scores = jnp.einsum('aw,kwe->ake', trunk_features.astype(jnp.float32), emission_head_weight.astype(jnp.float32))

    def forward_step(carry_vec, emit_row):
        updated = emit_row + jax.nn.logsumexp(carry_vec[:, :, None] + transitions, axis=1)
        updated = updated - lax.optimization_barrier(jnp.max(updated, axis=1, keepdims=True))
        return (updated, updated)

    def backward_step(carry_vec, emit_row):
        earlier = jax.nn.logsumexp(transitions + (emit_row + carry_vec)[:, None, :], axis=2)
        earlier = earlier - lax.optimization_barrier(jnp.max(earlier, axis=1, keepdims=True))
        return (earlier, carry_vec)
    start_vec = jnp.zeros((TISSUE_TYPES, LABEL_COUNT), jnp.float32)
    _, alpha_all = lax.scan(forward_step, start_vec, emission_scores)
    _, beta_all = lax.scan(backward_step, start_vec, emission_scores, reverse=True)
    joint_log = alpha_all + beta_all
    result = jnp.maximum(joint_log - jax.nn.logsumexp(joint_log, axis=2, keepdims=True), -30.0)
    return jnp.transpose(result, (1, 0, 2))
```

```python
import functools

import jax
import jax.numpy as jnp
from jax import lax
from jax.experimental import pallas as pl
from jax.experimental.pallas import tpu as pltpu
from jax.sharding import PartitionSpec as P

BIN_BP = 128
BASE_DILATION = 4
SUB = 8
MESH = pl.DeviceIdType.MESH
F32 = jnp.float32
BF16 = jnp.bfloat16


def halves(x):
    hi = x.astype(BF16).astype(F32)
    return hi, x - hi


def beside(x):
    hi, lo = halves(x)
    return jnp.concatenate([hi.astype(BF16), lo.astype(BF16)], axis=1)


def above(x):
    hi, lo = halves(x)
    return jnp.concatenate([hi, lo], axis=0).astype(BF16)


def row_times(stacked, pair):
    n = pair.shape[1] // 2
    y = jnp.dot(stacked, pair, preferred_element_type=F32)
    y = y[:, :n] + y[:, n:]
    half = y.shape[0] // 2
    return y[:half] + y[half:]


def row_times_t(stacked, pair):
    y = lax.dot_general(
        jnp.concatenate([stacked, stacked], axis=1),
        pair,
        (((1,), (1,)), ((), ())),
        preferred_element_type=F32,
    )
    half = y.shape[0] // 2
    return y[:half] + y[half:]


def unit_rows(v):
    return v / jnp.max(v, axis=-1, keepdims=True)


def top(x):
    return jnp.max(jnp.max(x, axis=-1, keepdims=True), axis=-2, keepdims=True)


def crf_kernel(
    feat_ref, head_ref, trans_ref, out_ref,
    f_ref, pair_ref, flip_ref, tree_ref, vin, win, vgot, wgot, vout, wout, st_ref, af_ref,
    al_ref, be_ref, ssem, rsem,
):
    cells, states = head_ref.shape[0], head_ref.shape[2]
    bins = feat_ref.shape[0]
    count = bins // SUB
    n = lax.axis_size("seq")
    me = lax.axis_index("seq")

    if n > 1:
        barrier = pltpu.get_barrier_semaphore()

        @pl.when(me > 0)
        def _():
            pl.semaphore_signal(barrier, inc=1, device_id={"seq": me - 1}, device_id_type=MESH)

        @pl.when(me < n - 1)
        def _():
            pl.semaphore_signal(barrier, inc=1, device_id={"seq": me + 1}, device_id_type=MESH)

        inner = jnp.logical_and(me > 0, me < n - 1)
        pl.semaphore_wait(barrier, jnp.where(inner, 2, 1))

    def chain(c, _):
        scores = jnp.dot(feat_ref[...], head_ref[c], preferred_element_type=F32)
        f_ref[c] = jnp.exp(scores - jnp.max(scores, axis=1, keepdims=True))
        raw = trans_ref[c]
        t = jnp.exp(raw - top(raw))
        pair = beside(t)
        pair_ref[c] = pair
        flip_ref[c] = beside(t.T)
        twice = jnp.concatenate([pair, pair], axis=0)
        x = t[None] * f_ref[c, pl.ds(0, count, stride=SUB), :][:, None, :]
        for j in range(1, SUB):
            scale = 1.0 / top(x)
            g = f_ref[c, pl.ds(j, count, stride=SUB), :][:, None, :] * scale
            y = jnp.dot(
                beside(x.reshape(count * states, states)), twice, preferred_element_type=F32
            )
            x = (y[:, :states] + y[:, states:]).reshape(count, states, states) * g
        x = x * (1.0 / top(x))
        nodes = []
        for k in range(count):
            nodes.append(beside(x[k]))
            tree_ref[c, k] = nodes[k]
        place = count
        while len(nodes) > 1:
            joined = []
            for k in range(0, len(nodes), 2):
                right = jnp.concatenate([nodes[k + 1], nodes[k + 1]], axis=0)
                y = jnp.dot(nodes[k], right, preferred_element_type=F32)
                y = y[:, :states] + y[:, states:]
                node = beside(y * (1.0 / top(y)))
                tree_ref[c, place] = node
                place += 1
                joined.append(node)
            nodes = joined
        return 0

    lax.fori_loop(0, cells, chain, 0)

    rows = lax.broadcasted_iota(jnp.int32, (cells, states), 0)

    def through(v, node, times):
        stacked = above(v)
        out = jnp.zeros_like(v)
        for c in range(cells):
            out = jnp.where(rows == c, times(stacked, tree_ref[c, node]), out)
        return unit_rows(out)

    whole = 2 * count - 2

    def forward_carry():
        @pl.when(me == 0)
        def _():
            vin[...] = jnp.ones_like(vin)

        @pl.when(me > 0)
        def _():
            pltpu.make_async_remote_copy(
                vout, vgot, ssem.at[0], rsem.at[0], device_id={"seq": me - 1}, device_id_type=MESH
            ).wait_recv()
            vin[...] = vgot[...]

        @pl.when(me < n - 1)
        def _():
            vout[...] = through(vin[...], whole, row_times)
            pltpu.make_async_remote_copy(
                vout, vgot, ssem.at[0], rsem.at[0], device_id={"seq": me + 1}, device_id_type=MESH
            ).start()

    def backward_carry():
        @pl.when(me == n - 1)
        def _():
            win[...] = jnp.ones_like(win)

        @pl.when(me < n - 1)
        def _():
            pltpu.make_async_remote_copy(
                wout, wgot, ssem.at[1], rsem.at[1], device_id={"seq": me + 1}, device_id_type=MESH
            ).wait_recv()
            win[...] = wgot[...]

        @pl.when(me > 0)
        def _():
            wout[...] = through(win[...], whole, row_times_t)
            pltpu.make_async_remote_copy(
                wout, wgot, ssem.at[1], rsem.at[1], device_id={"seq": me - 1}, device_id_type=MESH
            ).start()

    if n > 1:
        @pl.when(2 * me < n)
        def _():
            forward_carry()
            backward_carry()

        @pl.when(2 * me >= n)
        def _():
            backward_carry()
            forward_carry()
    else:
        vin[...] = jnp.ones_like(vin)
        win[...] = jnp.ones_like(win)

    starts = {0: vin[...]}
    afters = {count - 1: win[...]}
    width = count // 2
    base = 2 * count - 4
    while width >= 1:
        for k in range(0, count, 2 * width):
            starts[k + width] = through(starts[k], base + k // width, row_times)
            end = k + 2 * width - 1
            afters[end - width] = through(afters[end], base + end // width, row_times_t)
        width //= 2
        if width:
            base -= count // width
    for k in range(count):
        st_ref[pl.ds(k * cells, cells), :] = starts[k]
        af_ref[pl.ds(k * cells, cells), :] = afters[k]

    ahead = [st_ref[pl.ds(c, count, stride=cells), :] for c in range(cells)]
    behind = [af_ref[pl.ds(c, count, stride=cells), :] for c in range(cells)]
    for j in range(SUB):
        i = SUB - 1 - j
        for c in range(cells):
            fj = f_ref[c, pl.ds(j, count, stride=SUB), :]
            v = row_times(above(ahead[c]), pair_ref[c]) * fj
            v = unit_rows(v)
            al_ref[c, pl.ds(j * count, count), :] = v
            ahead[c] = v
            be_ref[c, pl.ds(i * count, count), :] = behind[c]
            if i > 0:
                fi = f_ref[c, pl.ds(i, count, stride=SUB), :]
                behind[c] = unit_rows(row_times(above(behind[c] * fi), flip_ref[c]))
    for c in range(cells):
        joint = jnp.log(al_ref[c]) + jnp.log(be_ref[c])
        peak = jnp.max(joint, axis=1, keepdims=True)
        total = jnp.log(jnp.sum(jnp.exp(joint - peak), axis=1, keepdims=True))
        result = jnp.maximum(joint - peak - total, -30.0)
        for j in range(SUB):
            out_ref[c, pl.ds(j, count, stride=SUB), :] = result[j * count : (j + 1) * count]

    if n > 1:
        @pl.when(me < n - 1)
        def _():
            pltpu.make_async_remote_copy(
                vout, vgot, ssem.at[0], rsem.at[0], device_id={"seq": me + 1}, device_id_type=MESH
            ).wait_send()

        @pl.when(me > 0)
        def _():
            pltpu.make_async_remote_copy(
                wout, wgot, ssem.at[1], rsem.at[1], device_id={"seq": me - 1}, device_id_type=MESH
            ).wait_send()


def crf(features, heads, transitions):
    bins = features.shape[0]
    cells, _, states = heads.shape
    count = bins // SUB
    vmem = pl.BlockSpec(memory_space=pltpu.VMEM)
    vec = pltpu.VMEM((cells, states), F32)
    return pl.pallas_call(
        crf_kernel,
        name="crf",
        out_shape=jax.ShapeDtypeStruct((cells, bins, states), F32),
        in_specs=[vmem] * 3,
        out_specs=vmem,
        scratch_shapes=[
            pltpu.VMEM((cells, bins, states), F32),
            pltpu.VMEM((cells, states, 2 * states), BF16),
            pltpu.VMEM((cells, states, 2 * states), BF16),
            pltpu.VMEM((cells, 2 * count - 1, states, 2 * states), BF16),
            vec, vec, vec, vec, vec, vec,
            pltpu.VMEM((count * cells, states), F32),
            pltpu.VMEM((count * cells, states), F32),
            pltpu.VMEM((cells, bins, states), F32),
            pltpu.VMEM((cells, bins, states), F32),
            pltpu.SemaphoreType.DMA((2,)),
            pltpu.SemaphoreType.DMA((2,)),
        ],
        compiler_params=pltpu.CompilerParams(
            collective_id=1, has_side_effects=True, vmem_limit_bytes=40 << 20
        ),
    )(features, heads, transitions)


def with_halo(block, sides, width):
    for axis, dim in sides:
        count = lax.axis_size(axis)
        forward = [(i, i + 1) for i in range(count - 1)]
        backward = [(target, source) for source, target in forward]
        low = lax.ppermute(
            lax.slice_in_dim(block, block.shape[dim] - width, None, axis=dim), axis, forward
        )
        high = lax.ppermute(lax.slice_in_dim(block, 0, width, axis=dim), axis, backward)
        block = jnp.concatenate([low, block, high], axis=dim)
    return block


def scaled(values):
    return values * lax.rsqrt(jnp.mean(values * values, axis=-1, keepdims=True) + 1e-06)


def tap_stack(conv_input, spacing_multiplier):
    out_rows = conv_input.shape[0] - 2 * spacing_multiplier
    return jnp.concatenate(
        [
            conv_input[0:out_rows],
            conv_input[spacing_multiplier : spacing_multiplier + out_rows],
            conv_input[2 * spacing_multiplier : 2 * spacing_multiplier + out_rows],
        ],
        axis=1,
    )


def branch(stacked, conv_slice, proj_slice):
    flat_weight = conv_slice.reshape(conv_slice.shape[0], -1)
    conv_out = lax.dot_general(
        stacked, flat_weight, (((1,), (1,)), ((), ())), preferred_element_type=jnp.float32
    )
    hidden = jax.nn.gelu(conv_out).astype(jnp.bfloat16)
    partial_value = jnp.dot(hidden, proj_slice, preferred_element_type=jnp.float32)
    return lax.psum(partial_value.astype(jnp.bfloat16), "cell").astype(jnp.float32)


def per_device(dna_bases, stem_weight, conv_weight, proj_weight, emission_head_weight, transitions):
    bin_rows = dna_bases.shape[0] // BIN_BP
    base_hits = dna_bases.reshape(bin_rows, BIN_BP, 1) == jnp.arange(4, dtype=jnp.int32)
    one_hot = base_hits.astype(jnp.bfloat16).reshape(bin_rows, BIN_BP * 4)
    stem_out = jnp.dot(one_hot, stem_weight, preferred_element_type=jnp.float32).astype(
        jnp.bfloat16
    )
    layers = conv_weight.shape[0]
    residual = stem_out.astype(jnp.float32)
    for layer_position in range(layers):
        spacing_multiplier = BASE_DILATION * 2**layer_position
        conv_input = jax.nn.gelu(scaled(residual)).astype(jnp.bfloat16)
        widened = with_halo(conv_input, (("seq", 0),), spacing_multiplier)
        residual = residual + branch(
            tap_stack(widened, spacing_multiplier),
            conv_weight[layer_position],
            proj_weight[layer_position],
        )
    trunk_features = scaled(residual).astype(jnp.bfloat16)
    return crf(trunk_features, emission_head_weight, transitions)


def solution(mesh):
    placed = (
        P(("groups", "seq")),
        P(),
        P(None, "cell", None, None),
        P(None, "cell", None),
        P("cell", None, None),
        P("cell", None, None),
    )
    return jax.shard_map(
        per_device,
        mesh=mesh,
        in_specs=placed,
        out_specs=P("cell", ("groups", "seq"), None),
        check_vma=False,
    )
```

```python
import functools

import jax
import jax.numpy as jnp
from jax import lax
from jax.experimental import pallas as pl
from jax.experimental.pallas import tpu as pltpu
from jax.sharding import PartitionSpec as P

BIN_BP = 128
BASE_DILATION = 4
SUB = 8
HALO = 16
MESH = pl.DeviceIdType.MESH
F32 = jnp.float32
BF16 = jnp.bfloat16


def halves(x):
    hi = x.astype(BF16).astype(F32)
    return hi, x - hi


def beside(x):
    hi, lo = halves(x)
    return jnp.concatenate([hi.astype(BF16), lo.astype(BF16)], axis=1)


def above(x):
    hi, lo = halves(x)
    return jnp.concatenate([hi, lo], axis=0).astype(BF16)


def row_times(stacked, pair):
    n = pair.shape[1] // 2
    y = jnp.dot(stacked, pair, preferred_element_type=F32)
    y = y[:, :n] + y[:, n:]
    half = y.shape[0] // 2
    return y[:half] + y[half:]


def row_times_t(stacked, pair):
    y = lax.dot_general(
        jnp.concatenate([stacked, stacked], axis=1),
        pair,
        (((1,), (1,)), ((), ())),
        preferred_element_type=F32,
    )
    half = y.shape[0] // 2
    return y[:half] + y[half:]


def unit_rows(v):
    return v / jnp.max(v, axis=-1, keepdims=True)


def top(x):
    return jnp.max(jnp.max(x, axis=-1, keepdims=True), axis=-2, keepdims=True)


def rms(v):
    return v * lax.rsqrt(jnp.mean(v * v, axis=-1, keepdims=True) + 1e-06)


def crf_kernel(
    bases_ref, stem_hbm, conv_hbm, proj_ref, head_hbm, trans_ref, out_ref,
    stem_ref, conv_ref, head_ref, lsem,
    wide_ref, wts_ref, gath_ref, hs_sem, hr_sem, ws_sem, wr_sem, gs_sem, gr_sem, feat_ref,
    f_ref, trn_ref, pair_ref, flip_ref, tree_ref, vin, win, vgot, wgot, vout, wout, st_ref,
    af_ref, al_ref, be_ref, ssem, rsem,
):
    cells, states = head_ref.shape[0], head_ref.shape[2]
    bins = feat_ref.shape[0]
    count = bins // SUB
    layers = conv_ref.shape[0]
    rows_wide = bins + 2 * HALO
    n = lax.axis_size("seq")
    me = lax.axis_index("seq")
    cell = lax.axis_index("cell")
    near = cell + 1 - 2 * (cell % 2)
    far = (cell + 2) % 4
    diag = (near + 2) % 4
    peers = (None, near, far, diag)

    loads = [
        pltpu.make_async_copy(src, dst, lsem.at[i])
        for i, (src, dst) in enumerate(
            [(stem_hbm, stem_ref), (conv_hbm, conv_ref), (head_hbm, head_ref)]
        )
    ]
    for load in loads:
        load.start()

    barrier = pltpu.get_barrier_semaphore()
    for peer in peers[1:]:
        pl.semaphore_signal(barrier, inc=1, device_id={"cell": peer}, device_id_type=MESH)

    @pl.when(me > 0)
    def _():
        pl.semaphore_signal(barrier, inc=1, device_id={"seq": me - 1}, device_id_type=MESH)

    @pl.when(me < n - 1)
    def _():
        pl.semaphore_signal(barrier, inc=1, device_id={"seq": me + 1}, device_id_type=MESH)

    inner = jnp.logical_and(me > 0, me < n - 1)
    pl.semaphore_wait(barrier, jnp.where(inner, 5, 4 if n > 1 else 3))

    upward = pltpu.make_async_remote_copy(
        bases_ref.at[pl.ds(bins - HALO, HALO)], wide_ref.at[pl.ds(0, HALO)],
        hs_sem.at[0], hr_sem.at[0],
        device_id={"seq": jnp.minimum(me + 1, n - 1)}, device_id_type=MESH,
    )
    downward = pltpu.make_async_remote_copy(
        bases_ref.at[pl.ds(0, HALO)], wide_ref.at[pl.ds(HALO, HALO)],
        hs_sem.at[1], hr_sem.at[1],
        device_id={"seq": jnp.maximum(me - 1, 0)}, device_id_type=MESH,
    )

    @pl.when(me < n - 1)
    def _():
        upward.start()

    @pl.when(me > 0)
    def _():
        downward.start()

    def send_weight(layer, k):
        own = pl.ds(0, proj_ref.shape[1])
        source = wts_ref.at[layer, 2, own] if k == 3 else proj_ref.at[layer]
        return pltpu.make_async_remote_copy(
            source, wts_ref.at[layer, k, own], ws_sem.at[layer, k], wr_sem.at[layer, k],
            device_id={"cell": far if k == 2 else near}, device_id_type=MESH,
        )

    def send_hidden(layer, k):
        return pltpu.make_async_remote_copy(
            gath_ref.at[layer, 0], gath_ref.at[layer, k], gs_sem.at[layer, k],
            gr_sem.at[layer, k], device_id={"cell": peers[k]}, device_id_type=MESH,
        )

    for layer in range(layers):
        send_weight(layer, 2).start()
        send_weight(layer, 1).start()
    held, padded = proj_ref.shape[1], wts_ref.shape[2]
    for layer in range(layers):
        wts_ref[layer, 0, pl.ds(0, held), :] = proj_ref[layer]
        if padded > held:
            for k in range(4):
                wts_ref[layer, k, pl.ds(held, padded - held), :] = jnp.zeros(
                    (padded - held, wts_ref.shape[3]), BF16
                )

    def prepare(c, _):
        raw = trans_ref[c]
        t = jnp.exp(raw - top(raw))
        trn_ref[c] = t
        pair_ref[c] = beside(t)
        flip_ref[c] = beside(t.T)
        return 0

    lax.fori_loop(0, cells // 2, prepare, 0)

    columns = lax.broadcasted_iota(jnp.int32, (BIN_BP, 4 * BIN_BP), 1)
    spread = (columns // 4 == lax.broadcasted_iota(jnp.int32, columns.shape, 0)).astype(BF16)

    @pl.when(me > 0)
    def _():
        upward.wait_recv()

    @pl.when(me == 0)
    def _():
        wide_ref[pl.ds(0, HALO), :] = jnp.zeros((HALO, BIN_BP), jnp.int32)

    @pl.when(me < n - 1)
    def _():
        downward.wait_recv()

    @pl.when(me == n - 1)
    def _():
        wide_ref[pl.ds(HALO, HALO), :] = jnp.zeros((HALO, BIN_BP), jnp.int32)

    bases = jnp.concatenate(
        [wide_ref[pl.ds(0, HALO), :], bases_ref[...], wide_ref[pl.ds(HALO, HALO), :]], axis=0
    )
    repeated = jnp.dot(
        bases.astype(F32).astype(BF16), spread, preferred_element_type=F32
    )
    which = (lax.broadcasted_iota(jnp.int32, repeated.shape, 1) % 4).astype(F32)
    one_hot = jnp.where(repeated == which, 1.0, 0.0).astype(BF16)
    loads[0].wait()
    residual = jnp.dot(one_hot, stem_ref[...], preferred_element_type=F32).astype(BF16).astype(F32)
    place = lax.broadcasted_iota(jnp.int32, residual.shape, 0) + (me * bins - HALO)
    inside = jnp.logical_and(place >= 0, place < n * bins)
    loads[1].wait()
    for layer in range(layers):
        dilation = BASE_DILATION * 2**layer
        conv_in = jnp.where(inside, jax.nn.gelu(rms(residual)), 0.0).astype(BF16)
        taps = [
            lax.dot_general(
                conv_in, conv_ref[layer, k], (((1,), (1,)), ((), ())), preferred_element_type=F32
            )
            for k in range(3)
        ]
        conv_out = (
            pltpu.roll(taps[0], dilation, 0)
            + taps[1]
            + pltpu.roll(taps[2], rows_wide - dilation, 0)
        )
        gath_ref[layer, 0] = jax.nn.gelu(conv_out).astype(BF16)
        for k in (2, 3, 1):
            send_hidden(layer, k).start()
        send_weight(layer, 2).wait_recv()
        send_weight(layer, 3).start()
        if layer == 0:
            lax.fori_loop(cells // 2, cells, prepare, 0)
        for k in (1, 2, 3):
            if k != 2:
                send_weight(layer, k).wait_recv()
            send_hidden(layer, k).wait_recv()
        hidden = jnp.concatenate([gath_ref[layer, k] for k in range(4)], axis=1)
        residual = residual + jnp.dot(
            hidden,
            wts_ref[layer].reshape(4 * padded, wts_ref.shape[3]),
            preferred_element_type=F32,
        )
    feat_ref[...] = rms(residual[HALO : HALO + bins]).astype(BF16)
    loads[2].wait()

    def chain(c, _):
        scores = jnp.dot(feat_ref[...], head_ref[c], preferred_element_type=F32)
        f_ref[c] = jnp.exp(scores - jnp.max(scores, axis=1, keepdims=True))
        t = trn_ref[c]
        pair = pair_ref[c]
        twice = jnp.concatenate([pair, pair], axis=0)
        x = t[None] * f_ref[c, pl.ds(0, count, stride=SUB), :][:, None, :]
        for j in range(1, SUB):
            scale = 1.0 / top(x)
            g = f_ref[c, pl.ds(j, count, stride=SUB), :][:, None, :] * scale
            y = jnp.dot(
                beside(x.reshape(count * states, states)), twice, preferred_element_type=F32
            )
            x = (y[:, :states] + y[:, states:]).reshape(count, states, states) * g
        x = x * (1.0 / top(x))
        nodes = []
        for k in range(count):
            nodes.append(beside(x[k]))
            tree_ref[c, k] = nodes[k]
        place = count
        while len(nodes) > 1:
            joined = []
            for k in range(0, len(nodes), 2):
                right = jnp.concatenate([nodes[k + 1], nodes[k + 1]], axis=0)
                y = jnp.dot(nodes[k], right, preferred_element_type=F32)
                y = y[:, :states] + y[:, states:]
                node = beside(y * (1.0 / top(y)))
                tree_ref[c, place] = node
                place += 1
                joined.append(node)
            nodes = joined
        return 0

    lax.fori_loop(0, cells, chain, 0)

    rows = lax.broadcasted_iota(jnp.int32, (cells, states), 0)

    def through(v, node, times):
        stacked = above(v)
        out = jnp.zeros_like(v)
        for c in range(cells):
            out = jnp.where(rows == c, times(stacked, tree_ref[c, node]), out)
        return unit_rows(out)

    whole = 2 * count - 2

    def forward_carry():
        @pl.when(me == 0)
        def _():
            vin[...] = jnp.ones_like(vin)

        @pl.when(me > 0)
        def _():
            pltpu.make_async_remote_copy(
                vout, vgot, ssem.at[0], rsem.at[0], device_id={"seq": me - 1}, device_id_type=MESH
            ).wait_recv()
            vin[...] = vgot[...]

        @pl.when(me < n - 1)
        def _():
            vout[...] = through(vin[...], whole, row_times)
            pltpu.make_async_remote_copy(
                vout, vgot, ssem.at[0], rsem.at[0], device_id={"seq": me + 1}, device_id_type=MESH
            ).start()

    def backward_carry():
        @pl.when(me == n - 1)
        def _():
            win[...] = jnp.ones_like(win)

        @pl.when(me < n - 1)
        def _():
            pltpu.make_async_remote_copy(
                wout, wgot, ssem.at[1], rsem.at[1], device_id={"seq": me + 1}, device_id_type=MESH
            ).wait_recv()
            win[...] = wgot[...]

        @pl.when(me > 0)
        def _():
            wout[...] = through(win[...], whole, row_times_t)
            pltpu.make_async_remote_copy(
                wout, wgot, ssem.at[1], rsem.at[1], device_id={"seq": me - 1}, device_id_type=MESH
            ).start()

    if n > 1:
        @pl.when(2 * me < n)
        def _():
            forward_carry()
            backward_carry()

        @pl.when(2 * me >= n)
        def _():
            backward_carry()
            forward_carry()
    else:
        vin[...] = jnp.ones_like(vin)
        win[...] = jnp.ones_like(win)

    starts = {0: vin[...]}
    afters = {count - 1: win[...]}
    width = count // 2
    base = 2 * count - 4
    while width >= 1:
        for k in range(0, count, 2 * width):
            starts[k + width] = through(starts[k], base + k // width, row_times)
            end = k + 2 * width - 1
            afters[end - width] = through(afters[end], base + end // width, row_times_t)
        width //= 2
        if width:
            base -= count // width
    for k in range(count):
        st_ref[pl.ds(k * cells, cells), :] = starts[k]
        af_ref[pl.ds(k * cells, cells), :] = afters[k]

    ahead = [st_ref[pl.ds(c, count, stride=cells), :] for c in range(cells)]
    behind = [af_ref[pl.ds(c, count, stride=cells), :] for c in range(cells)]
    for j in range(SUB):
        i = SUB - 1 - j
        for c in range(cells):
            fj = f_ref[c, pl.ds(j, count, stride=SUB), :]
            v = row_times(above(ahead[c]), pair_ref[c]) * fj
            v = unit_rows(v)
            al_ref[c, pl.ds(j * count, count), :] = v
            ahead[c] = v
            be_ref[c, pl.ds(i * count, count), :] = behind[c]
            if i > 0:
                fi = f_ref[c, pl.ds(i, count, stride=SUB), :]
                behind[c] = unit_rows(row_times(above(behind[c] * fi), flip_ref[c]))
    for c in range(cells):
        joint = jnp.log(al_ref[c]) + jnp.log(be_ref[c])
        peak = jnp.max(joint, axis=1, keepdims=True)
        total = jnp.log(jnp.sum(jnp.exp(joint - peak), axis=1, keepdims=True))
        result = jnp.maximum(joint - peak - total, -30.0)
        for j in range(SUB):
            out_ref[c, pl.ds(j, count, stride=SUB), :] = result[j * count : (j + 1) * count]

    if n > 1:
        @pl.when(me < n - 1)
        def _():
            pltpu.make_async_remote_copy(
                vout, vgot, ssem.at[0], rsem.at[0], device_id={"seq": me + 1}, device_id_type=MESH
            ).wait_send()

        @pl.when(me > 0)
        def _():
            pltpu.make_async_remote_copy(
                wout, wgot, ssem.at[1], rsem.at[1], device_id={"seq": me - 1}, device_id_type=MESH
            ).wait_send()

    @pl.when(me < n - 1)
    def _():
        upward.wait_send()

    @pl.when(me > 0)
    def _():
        downward.wait_send()

    for layer in range(layers):
        for k in (1, 2, 3):
            send_weight(layer, k).wait_send()
            send_hidden(layer, k).wait_send()


def per_device(dna_bases, stem_weight, conv_weight, proj_weight, emission_head_weight, transitions):
    bins = dna_bases.shape[0] // BIN_BP
    cells, _, states = emission_head_weight.shape
    layers, held, taps, wide = conv_weight.shape
    inner = pl.cdiv(held, 128) * 128
    count = bins // SUB
    assert HALO >= BASE_DILATION * (2**layers - 1) and lax.axis_size("cell") == 4
    rows = bins + 2 * HALO
    vmem = pl.BlockSpec(memory_space=pltpu.VMEM)
    hbm = pl.BlockSpec(memory_space=pl.ANY)
    vec = pltpu.VMEM((cells, states), F32)
    dma = pltpu.SemaphoreType.DMA
    return pl.pallas_call(
        crf_kernel,
        name="crf",
        out_shape=jax.ShapeDtypeStruct((cells, bins, states), F32),
        in_specs=[vmem, hbm, hbm, vmem, hbm, vmem],
        out_specs=vmem,
        scratch_shapes=[
            pltpu.VMEM(stem_weight.shape, BF16),
            pltpu.VMEM((layers, taps, inner, wide), BF16),
            pltpu.VMEM(emission_head_weight.shape, BF16),
            dma((3,)),
            pltpu.VMEM((2 * HALO, BIN_BP), jnp.int32),
            pltpu.VMEM((layers, 4, inner, wide), BF16),
            pltpu.VMEM((layers, 4, rows, inner), BF16),
            dma((2,)), dma((2,)),
            dma((layers, 4)), dma((layers, 4)), dma((layers, 4)), dma((layers, 4)),
            pltpu.VMEM((bins, wide), BF16),
            pltpu.VMEM((cells, bins, states), F32),
            pltpu.VMEM((cells, states, states), F32),
            pltpu.VMEM((cells, states, 2 * states), BF16),
            pltpu.VMEM((cells, states, 2 * states), BF16),
            pltpu.VMEM((cells, 2 * count - 1, states, 2 * states), BF16),
            vec, vec, vec, vec, vec, vec,
            pltpu.VMEM((count * cells, states), F32),
            pltpu.VMEM((count * cells, states), F32),
            pltpu.VMEM((cells, bins, states), F32),
            pltpu.VMEM((cells, bins, states), F32),
            dma((2,)), dma((2,)),
        ],
        compiler_params=pltpu.CompilerParams(
            collective_id=1, has_side_effects=True, vmem_limit_bytes=48 << 20
        ),
    )(
        dna_bases.reshape(bins, BIN_BP),
        stem_weight,
        jnp.pad(conv_weight.transpose(0, 2, 1, 3), ((0, 0), (0, 0), (0, inner - held), (0, 0))),
        proj_weight,
        emission_head_weight,
        transitions,
    )


def solution(mesh):
    placed = (
        P(("groups", "seq")),
        P(),
        P(None, "cell", None, None),
        P(None, "cell", None),
        P("cell", None, None),
        P("cell", None, None),
    )
    return jax.shard_map(
        per_device,
        mesh=mesh,
        in_specs=placed,
        out_specs=P("cell", ("groups", "seq"), None),
        check_vma=False,
    )
```

```python
import functools

import jax
import jax.numpy as jnp
from jax import lax
from jax.experimental import pallas as pl
from jax.experimental.pallas import tpu as pltpu
from jax.sharding import PartitionSpec as P

BIN_BP = 128
BASE_DILATION = 4
SUB = 8
HALO = 16
WIDTH = 4
MESH = pl.DeviceIdType.MESH
F32 = jnp.float32
BF16 = jnp.bfloat16


def halves(x):
    hi = x.astype(BF16).astype(F32)
    return hi, x - hi


def beside(x):
    hi, lo = halves(x)
    return jnp.concatenate([hi.astype(BF16), lo.astype(BF16)], axis=1)


def above(x):
    hi, lo = halves(x)
    return jnp.concatenate([hi, lo], axis=0).astype(BF16)


def row_times(stacked, pair):
    n = pair.shape[1] // 2
    y = jnp.dot(stacked, pair, preferred_element_type=F32)
    y = y[:, :n] + y[:, n:]
    half = y.shape[0] // 2
    return y[:half] + y[half:]


def row_times_t(stacked, pair):
    y = lax.dot_general(
        jnp.concatenate([stacked, stacked], axis=1),
        pair,
        (((1,), (1,)), ((), ())),
        preferred_element_type=F32,
    )
    half = y.shape[0] // 2
    return y[:half] + y[half:]


def unit_rows(v):
    return v / jnp.max(v, axis=-1, keepdims=True)


def top(x):
    return jnp.max(jnp.max(x, axis=-1, keepdims=True), axis=-2, keepdims=True)


def rms(v):
    return v * lax.rsqrt(jnp.mean(v * v, axis=-1, keepdims=True) + 1e-06)


def crf_kernel(
    bases_ref, stem_hbm, conv_hbm, proj_ref, head_hbm, trans_ref, out_ref,
    stem_ref, conv_ref, head_ref, lsem,
    wide_ref, wts_ref, gath_ref, hs_sem, hr_sem, ws_sem, wr_sem, gs_sem, gr_sem, feat_ref,
    f_ref, trn_ref, pair_ref, flip_ref, tree_ref, vin, win, vgot, wgot, vout, wout, st_ref,
    af_ref, al_ref, be_ref, ssem, rsem,
):
    cells, states = head_ref.shape[0], head_ref.shape[2]
    bins = feat_ref.shape[0]
    count = bins // SUB
    layers = conv_ref.shape[0]
    rows_wide = bins + 2 * HALO
    n = lax.axis_size("seq")
    me = lax.axis_index("seq")
    cell = lax.axis_index("cell")
    near = cell + 1 - 2 * (cell % 2)
    far = (cell + 2) % 4
    diag = (near + 2) % 4
    peers = (None, near, far, diag)

    loads = [
        pltpu.make_async_copy(src, dst, lsem.at[i])
        for i, (src, dst) in enumerate(
            [(stem_hbm, stem_ref), (conv_hbm, conv_ref), (head_hbm, head_ref)]
        )
    ]
    for load in loads:
        load.start()

    barrier = pltpu.get_barrier_semaphore()
    for peer in peers[1:]:
        pl.semaphore_signal(barrier, inc=1, device_id={"cell": peer}, device_id_type=MESH)

    @pl.when(me > 0)
    def _():
        pl.semaphore_signal(barrier, inc=1, device_id={"seq": me - 1}, device_id_type=MESH)

    @pl.when(me < n - 1)
    def _():
        pl.semaphore_signal(barrier, inc=1, device_id={"seq": me + 1}, device_id_type=MESH)

    inner = jnp.logical_and(me > 0, me < n - 1)
    pl.semaphore_wait(barrier, jnp.where(inner, 5, 4 if n > 1 else 3))

    upward = pltpu.make_async_remote_copy(
        bases_ref.at[pl.ds(bins - HALO, HALO)], wide_ref.at[pl.ds(0, HALO)],
        hs_sem.at[0], hr_sem.at[0],
        device_id={"seq": jnp.minimum(me + 1, n - 1)}, device_id_type=MESH,
    )
    downward = pltpu.make_async_remote_copy(
        bases_ref.at[pl.ds(0, HALO)], wide_ref.at[pl.ds(HALO, HALO)],
        hs_sem.at[1], hr_sem.at[1],
        device_id={"seq": jnp.maximum(me - 1, 0)}, device_id_type=MESH,
    )

    @pl.when(me < n - 1)
    def _():
        upward.start()

    @pl.when(me > 0)
    def _():
        downward.start()

    def send_weight(layer, k):
        own = pl.ds(0, proj_ref.shape[1])
        source = wts_ref.at[layer, 2, own] if k == 3 else proj_ref.at[layer]
        return pltpu.make_async_remote_copy(
            source, wts_ref.at[layer, k, own], ws_sem.at[layer, k], wr_sem.at[layer, k],
            device_id={"cell": far if k == 2 else near}, device_id_type=MESH,
        )

    def send_hidden(layer, k):
        return pltpu.make_async_remote_copy(
            gath_ref.at[layer, 0], gath_ref.at[layer, k], gs_sem.at[layer, k],
            gr_sem.at[layer, k], device_id={"cell": peers[k]}, device_id_type=MESH,
        )

    for layer in range(layers):
        send_weight(layer, 2).start()
        send_weight(layer, 1).start()
    held, padded = proj_ref.shape[1], wts_ref.shape[2]
    for layer in range(layers):
        wts_ref[layer, 0, pl.ds(0, held), :] = proj_ref[layer]
        if padded > held:
            for k in range(4):
                wts_ref[layer, k, pl.ds(held, padded - held), :] = jnp.zeros(
                    (padded - held, wts_ref.shape[3]), BF16
                )

    def prepare(c, _):
        raw = trans_ref[c]
        t = jnp.exp(raw - top(raw))
        trn_ref[c] = t
        pair_ref[c] = beside(t)
        flip_ref[c] = beside(t.T)
        return 0

    lax.fori_loop(0, cells // 2, prepare, 0)

    columns = lax.broadcasted_iota(jnp.int32, (BIN_BP, 4 * BIN_BP), 1)
    spread = (columns // 4 == lax.broadcasted_iota(jnp.int32, columns.shape, 0)).astype(BF16)

    @pl.when(me > 0)
    def _():
        upward.wait_recv()

    @pl.when(me == 0)
    def _():
        wide_ref[pl.ds(0, HALO), :] = jnp.zeros((HALO, BIN_BP), jnp.int32)

    @pl.when(me < n - 1)
    def _():
        downward.wait_recv()

    @pl.when(me == n - 1)
    def _():
        wide_ref[pl.ds(HALO, HALO), :] = jnp.zeros((HALO, BIN_BP), jnp.int32)

    bases = jnp.concatenate(
        [wide_ref[pl.ds(0, HALO), :], bases_ref[...], wide_ref[pl.ds(HALO, HALO), :]], axis=0
    )
    repeated = jnp.dot(
        bases.astype(F32).astype(BF16), spread, preferred_element_type=F32
    )
    which = (lax.broadcasted_iota(jnp.int32, repeated.shape, 1) % 4).astype(F32)
    one_hot = jnp.where(repeated == which, 1.0, 0.0).astype(BF16)
    loads[0].wait()
    residual = jnp.dot(one_hot, stem_ref[...], preferred_element_type=F32).astype(BF16).astype(F32)
    place = lax.broadcasted_iota(jnp.int32, residual.shape, 0) + (me * bins - HALO)
    inside = jnp.logical_and(place >= 0, place < n * bins)
    loads[1].wait()
    for layer in range(layers):
        dilation = BASE_DILATION * 2**layer
        conv_in = jnp.where(inside, jax.nn.gelu(rms(residual)), 0.0).astype(BF16)
        taps = [
            lax.dot_general(
                conv_in, conv_ref[layer, k], (((1,), (1,)), ((), ())), preferred_element_type=F32
            )
            for k in range(3)
        ]
        conv_out = (
            pltpu.roll(taps[0], dilation, 0)
            + taps[1]
            + pltpu.roll(taps[2], rows_wide - dilation, 0)
        )
        gath_ref[layer, 0] = jax.nn.gelu(conv_out).astype(BF16)
        for k in (2, 3, 1):
            send_hidden(layer, k).start()
        send_weight(layer, 2).wait_recv()
        send_weight(layer, 3).start()
        if layer == 0:
            lax.fori_loop(cells // 2, cells, prepare, 0)
        for k in (1, 2, 3):
            if k != 2:
                send_weight(layer, k).wait_recv()
            send_hidden(layer, k).wait_recv()
        hidden = jnp.concatenate([gath_ref[layer, k] for k in range(4)], axis=1)
        residual = residual + jnp.dot(
            hidden,
            wts_ref[layer].reshape(4 * padded, wts_ref.shape[3]),
            preferred_element_type=F32,
        )
    feat_ref[...] = rms(residual[HALO : HALO + bins]).astype(BF16)
    loads[2].wait()

    def chain(i, _):
        group = [WIDTH * i + k for k in range(WIDTH)]
        scores = [jnp.dot(feat_ref[...], head_ref[c], preferred_element_type=F32) for c in group]
        for c, e in zip(group, scores):
            f_ref[c] = jnp.exp(e - jnp.max(e, axis=1, keepdims=True))
        twice = [jnp.concatenate([pair_ref[c], pair_ref[c]], axis=0) for c in group]
        xs = [
            trn_ref[c][None] * f_ref[c, pl.ds(0, count, stride=SUB), :][:, None, :] for c in group
        ]
        for j in range(1, SUB):
            for p, c in enumerate(group):
                x = xs[p]
                scale = 1.0 / top(x)
                g = f_ref[c, pl.ds(j, count, stride=SUB), :][:, None, :] * scale
                y = jnp.dot(
                    beside(x.reshape(count * states, states)),
                    twice[p],
                    preferred_element_type=F32,
                )
                xs[p] = (y[:, :states] + y[:, states:]).reshape(count, states, states) * g
        layers_of = []
        for p, c in enumerate(group):
            x = xs[p] * (1.0 / top(xs[p]))
            layers_of.append([beside(x[k]) for k in range(count)])
            for k in range(count):
                tree_ref[c, k] = layers_of[p][k]
        place = count
        while len(layers_of[0]) > 1:
            half = len(layers_of[0]) // 2
            for p, c in enumerate(group):
                nodes = layers_of[p]
                joined = []
                for k in range(half):
                    right = jnp.concatenate([nodes[2 * k + 1], nodes[2 * k + 1]], axis=0)
                    y = jnp.dot(nodes[2 * k], right, preferred_element_type=F32)
                    y = y[:, :states] + y[:, states:]
                    node = beside(y * (1.0 / top(y)))
                    tree_ref[c, place + k] = node
                    joined.append(node)
                layers_of[p] = joined
            place += half
        return 0

    lax.fori_loop(0, cells // WIDTH, chain, 0)

    rows = lax.broadcasted_iota(jnp.int32, (cells, states), 0)

    def through(v, node, times):
        stacked = above(v)
        out = jnp.zeros_like(v)
        for c in range(cells):
            out = jnp.where(rows == c, times(stacked, tree_ref[c, node]), out)
        return unit_rows(out)

    whole = 2 * count - 2

    def forward_carry():
        @pl.when(me == 0)
        def _():
            vin[...] = jnp.ones_like(vin)

        @pl.when(me > 0)
        def _():
            pltpu.make_async_remote_copy(
                vout, vgot, ssem.at[0], rsem.at[0], device_id={"seq": me - 1}, device_id_type=MESH
            ).wait_recv()
            vin[...] = vgot[...]

        @pl.when(me < n - 1)
        def _():
            vout[...] = through(vin[...], whole, row_times)
            pltpu.make_async_remote_copy(
                vout, vgot, ssem.at[0], rsem.at[0], device_id={"seq": me + 1}, device_id_type=MESH
            ).start()

    def backward_carry():
        @pl.when(me == n - 1)
        def _():
            win[...] = jnp.ones_like(win)

        @pl.when(me < n - 1)
        def _():
            pltpu.make_async_remote_copy(
                wout, wgot, ssem.at[1], rsem.at[1], device_id={"seq": me + 1}, device_id_type=MESH
            ).wait_recv()
            win[...] = wgot[...]

        @pl.when(me > 0)
        def _():
            wout[...] = through(win[...], whole, row_times_t)
            pltpu.make_async_remote_copy(
                wout, wgot, ssem.at[1], rsem.at[1], device_id={"seq": me - 1}, device_id_type=MESH
            ).start()

    if n > 1:
        @pl.when(2 * me < n)
        def _():
            forward_carry()
            backward_carry()

        @pl.when(2 * me >= n)
        def _():
            backward_carry()
            forward_carry()
    else:
        vin[...] = jnp.ones_like(vin)
        win[...] = jnp.ones_like(win)

    starts = {0: vin[...]}
    afters = {count - 1: win[...]}
    width = count // 2
    base = 2 * count - 4
    while width >= 1:
        for k in range(0, count, 2 * width):
            starts[k + width] = through(starts[k], base + k // width, row_times)
            end = k + 2 * width - 1
            afters[end - width] = through(afters[end], base + end // width, row_times_t)
        width //= 2
        if width:
            base -= count // width
    for k in range(count):
        st_ref[pl.ds(k * cells, cells), :] = starts[k]
        af_ref[pl.ds(k * cells, cells), :] = afters[k]

    ahead = [st_ref[pl.ds(c, count, stride=cells), :] for c in range(cells)]
    behind = [af_ref[pl.ds(c, count, stride=cells), :] for c in range(cells)]
    for j in range(SUB):
        i = SUB - 1 - j
        for c in range(cells):
            fj = f_ref[c, pl.ds(j, count, stride=SUB), :]
            v = row_times(above(ahead[c]), pair_ref[c]) * fj
            v = unit_rows(v)
            al_ref[c, pl.ds(j * count, count), :] = v
            ahead[c] = v
            be_ref[c, pl.ds(i * count, count), :] = behind[c]
            if i > 0:
                fi = f_ref[c, pl.ds(i, count, stride=SUB), :]
                behind[c] = unit_rows(row_times(above(behind[c] * fi), flip_ref[c]))
    for c in range(cells):
        joint = jnp.log(al_ref[c]) + jnp.log(be_ref[c])
        peak = jnp.max(joint, axis=1, keepdims=True)
        total = jnp.log(jnp.sum(jnp.exp(joint - peak), axis=1, keepdims=True))
        result = jnp.maximum(joint - peak - total, -30.0)
        for j in range(SUB):
            out_ref[c, pl.ds(j, count, stride=SUB), :] = result[j * count : (j + 1) * count]

    if n > 1:
        @pl.when(me < n - 1)
        def _():
            pltpu.make_async_remote_copy(
                vout, vgot, ssem.at[0], rsem.at[0], device_id={"seq": me + 1}, device_id_type=MESH
            ).wait_send()

        @pl.when(me > 0)
        def _():
            pltpu.make_async_remote_copy(
                wout, wgot, ssem.at[1], rsem.at[1], device_id={"seq": me - 1}, device_id_type=MESH
            ).wait_send()

    @pl.when(me < n - 1)
    def _():
        upward.wait_send()

    @pl.when(me > 0)
    def _():
        downward.wait_send()

    for layer in range(layers):
        for k in (1, 2, 3):
            send_weight(layer, k).wait_send()
            send_hidden(layer, k).wait_send()


def per_device(dna_bases, stem_weight, conv_weight, proj_weight, emission_head_weight, transitions):
    bins = dna_bases.shape[0] // BIN_BP
    cells, _, states = emission_head_weight.shape
    layers, held, taps, wide = conv_weight.shape
    inner = pl.cdiv(held, 128) * 128
    count = bins // SUB
    assert HALO >= BASE_DILATION * (2**layers - 1) and lax.axis_size("cell") == 4
    rows = bins + 2 * HALO
    vmem = pl.BlockSpec(memory_space=pltpu.VMEM)
    hbm = pl.BlockSpec(memory_space=pl.ANY)
    vec = pltpu.VMEM((cells, states), F32)
    dma = pltpu.SemaphoreType.DMA
    return pl.pallas_call(
        crf_kernel,
        name="crf",
        out_shape=jax.ShapeDtypeStruct((cells, bins, states), F32),
        in_specs=[vmem, hbm, hbm, vmem, hbm, vmem],
        out_specs=vmem,
        scratch_shapes=[
            pltpu.VMEM(stem_weight.shape, BF16),
            pltpu.VMEM((layers, taps, inner, wide), BF16),
            pltpu.VMEM(emission_head_weight.shape, BF16),
            dma((3,)),
            pltpu.VMEM((2 * HALO, BIN_BP), jnp.int32),
            pltpu.VMEM((layers, 4, inner, wide), BF16),
            pltpu.VMEM((layers, 4, rows, inner), BF16),
            dma((2,)), dma((2,)),
            dma((layers, 4)), dma((layers, 4)), dma((layers, 4)), dma((layers, 4)),
            pltpu.VMEM((bins, wide), BF16),
            pltpu.VMEM((cells, bins, states), F32),
            pltpu.VMEM((cells, states, states), F32),
            pltpu.VMEM((cells, states, 2 * states), BF16),
            pltpu.VMEM((cells, states, 2 * states), BF16),
            pltpu.VMEM((cells, 2 * count - 1, states, 2 * states), BF16),
            vec, vec, vec, vec, vec, vec,
            pltpu.VMEM((count * cells, states), F32),
            pltpu.VMEM((count * cells, states), F32),
            pltpu.VMEM((cells, bins, states), F32),
            pltpu.VMEM((cells, bins, states), F32),
            dma((2,)), dma((2,)),
        ],
        compiler_params=pltpu.CompilerParams(
            collective_id=1, has_side_effects=True, vmem_limit_bytes=48 << 20
        ),
    )(
        dna_bases.reshape(bins, BIN_BP),
        stem_weight,
        jnp.pad(conv_weight.transpose(0, 2, 1, 3), ((0, 0), (0, 0), (0, inner - held), (0, 0))),
        proj_weight,
        emission_head_weight,
        transitions,
    )


def solution(mesh):
    placed = (
        P(("groups", "seq")),
        P(),
        P(None, "cell", None, None),
        P(None, "cell", None),
        P("cell", None, None),
        P("cell", None, None),
    )
    return jax.shard_map(
        per_device,
        mesh=mesh,
        in_specs=placed,
        out_specs=P("cell", ("groups", "seq"), None),
        check_vma=False,
    )
```
